32 devices in a mesh: ta: 4 (over x, core), ha: 2 (over y), col: 4 (over z).
Axes of the slice: x: 2, y: 2, z: 4, core: 2. Of those that a mesh axis runs over, the one named last changes fastest.
Arguments:
- tokens: bfloat16 [8, 32, 14, 14, 512], P('col', 'ta', 'ha'), may hold values from -6 to 6
- qkv_weight: bfloat16 [512, 1536], P('col', ('ta', 'ha')), may hold values from -0.25 to 0.25
- query_bias: bfloat16 [512], P(('ta', 'ha')), may hold values from -2 to 2
- value_bias: bfloat16 [512], P(('ta', 'ha')), may hold values from -0.59765625 to 0.59765625
- proj_weight: bfloat16 [512, 512], P('col', ('ta', 'ha')), may hold values from -2 to 2
- proj_bias: bfloat16 [512], P(('ta', 'ha')), may hold values from -2 to 2
- fc1_weight: bfloat16 [512, 2048], P('col', ('ta', 'ha')), may hold values from -0.25 to 0.25
- fc1_bias: bfloat16 [2048], P(('ta', 'ha')), may hold values from -2 to 2
- fc2_weight: bfloat16 [2048, 512], P('col', ('ta', 'ha')), may hold values from -0.125 to 0.125
- fc2_bias: bfloat16 [512], P(('ta', 'ha')), may hold values from -2 to 2
- norm1_gain: bfloat16 [512], P(('ta', 'ha')), may hold values from 0.5 to 1.5
- norm1_shift: bfloat16 [512], P(('ta', 'ha')), may hold values from -1.1953125 to 1.1953125
- norm2_gain: bfloat16 [512], P(('ta', 'ha')), may hold values from 0.5 to 1.5
- norm2_shift: bfloat16 [512], P(('ta', 'ha')), may hold values from -1.1953125 to 1.1953125
- bias_table: bfloat16 [2535, 16], P(None, ('ta', 'ha')), may hold values from -3 to 3
- rel_index: int32 [392, 392], replicated, may hold values from 0 to 2534, as said below
- cotangent: bfloat16 [8, 32, 14, 14, 512], P('col', 'ta', 'ha'), may hold values from -6 to 6
Outputs:
- block_out: bfloat16 [8, 32, 14, 14, 512], P('col', 'ta', 'ha')
- tokens_grad: float32 [8, 32, 14, 14, 512], P('col', 'ta', 'ha')
- qkv_weight_grad: float32 [512, 1536], P(None, ('ta', 'ha'))
- query_bias_grad: float32 [512], P(('ta', 'ha'))
- value_bias_grad: float32 [512], P(('ta', 'ha'))
- proj_weight_grad: float32 [512, 512], P(None, ('ta', 'ha'))
- proj_bias_grad: float32 [512], P(('ta', 'ha'))
- fc1_weight_grad: float32 [512, 2048], P(None, ('ta', 'ha'))
- fc1_bias_grad: float32 [2048], P(('ta', 'ha'))
- fc2_weight_grad: float32 [2048, 512], P(None, ('ta', 'ha'))
- fc2_bias_grad: float32 [512], P(('ta', 'ha'))
- norm1_gain_grad: float32 [512], P(('ta', 'ha'))
- norm1_shift_grad: float32 [512], P(('ta', 'ha'))
- norm2_gain_grad: float32 [512], P(('ta', 'ha'))
- norm2_shift_grad: float32 [512], P(('ta', 'ha'))
- bias_table_grad: float32 [2535, 16], P(None, ('ta', 'ha'))
The draws below stay inside these ranges and needn't reach their ends.
Inputs may be any that keep to these rules, and one draw needn't show every extreme that they name: `rel_index`: entry (i, j) depends only on the differences of the frame, row and column of positions i and j inside a window, and distinct differences name distinct rows of bias_table.
All inputs are finite; a program needn't handle non-finite values.
Results may differ from the reference program's by a relative error of at most 0.012.
Values may be sent and summed in bfloat16 or wider, within the bound.
No kernel may reach another device: no remote copies, remote signals or barrier semaphores. Data moves between devices by JAX's collectives and lax.ppermute only.
A program may use at most 256 MiB of HBM per device.

```python
import jax
import jax.numpy as jnp
from jax import lax

D = 512
HEADS = 16
FF = 2048
WIN_T = 8
WIN_H = 7
WIN_W = 7
HEAD_DIM = 32
SHIFT_T = 4
SHIFT_H = 3
SHIFT_W = 3
WIDTH = 14
WIN = 392
RPB_ROWS = 2535
FRAMES = 32
HEIGHT = 14
CLIPS = 8


def draw_rel_index(key, part):
    position = jnp.arange(WIN, dtype=jnp.int32)
    frame_of = position // (WIN_H * WIN_W)
    row_of = position // WIN_W % WIN_H
    column_of = position % WIN_W
    frame_diff = frame_of[:, None] - frame_of[None, :] + WIN_T - 1
    row_diff = row_of[:, None] - row_of[None, :] + WIN_H - 1
    column_diff = column_of[:, None] - column_of[None, :] + WIN_W - 1
    canonical = (frame_diff * (2 * WIN_H - 1) + row_diff) * (2 * WIN_W - 1) + column_diff
    shuffled = jax.random.permutation(jax.random.fold_in(key, 7), RPB_ROWS).astype(jnp.int32)
    return shuffled[canonical].astype(jnp.int32)


def shard_levels(rng, dims, shards, low, high):
    def one(dim, blocks):
        steps = jax.random.uniform(jax.random.fold_in(jax.random.fold_in(rng, 6), dim), (blocks,), jnp.float32, low / len(shards), high / len(shards))
        return jnp.repeat(jnp.exp(steps), dims[dim] // blocks).reshape((-1,) + (1,) * (len(dims) - dim - 1))

    level = one(*shards[0])
    for cut in shards[1:]:
        level = level * one(*cut)
    return level


def noise(own_key, dims, deviation, bound, pieces=(), kind=jnp.bfloat16):
    loudness = shard_levels(own_key, dims, pieces, -0.22, 0.18) if pieces else 1.0
    array = jax.random.normal(own_key, dims, jnp.float32) * deviation * loudness
    return jnp.minimum(jnp.maximum(array, -bound), bound).astype(kind)


def setup_inputs(seed: int = 0) -> dict:
    arg_keys = jax.random.split(jax.random.key(seed), 18)
    return {
        "tokens": noise(arg_keys[0], (CLIPS, FRAMES, HEIGHT, WIDTH, D), 1.0, 6.0, ((0, 4), (1, 4), (2, 2))),
        "qkv_weight": noise(arg_keys[1], (D, 3 * D), D ** -0.5, 0.25, ((0, 4), (1, 8))),
        "query_bias": noise(arg_keys[2], (D,), 0.3, 2.0, ((0, 8),)),
        "value_bias": noise(arg_keys[3], (D,), 0.1, 0.59765625, ((0, 8),)),
        "proj_weight": noise(arg_keys[4], (D, D), (max(D // 64, 1)) ** -0.5, 2.0, ((0, 4), (1, 8))),
        "proj_bias": noise(arg_keys[5], (D,), 0.3, 2.0, ((0, 8),)),
        "fc1_weight": noise(arg_keys[6], (D, FF), D ** -0.5, 0.25, ((0, 4), (1, 8))),
        "fc1_bias": noise(arg_keys[7], (FF,), 0.3, 2.0, ((0, 8),)),
        "fc2_weight": noise(arg_keys[8], (FF, D), FF ** -0.5, 0.125, ((0, 4), (1, 8))),
        "fc2_bias": noise(arg_keys[9], (D,), 0.3, 2.0, ((0, 8),)),
        "norm1_gain": jnp.clip(1.0 + 0.1 * jax.random.normal(arg_keys[10], (D,), jnp.float32), 0.5, 1.5).astype(jnp.bfloat16),
        "norm1_shift": noise(arg_keys[11], (D,), 0.2, 1.1953125, ((0, 8),)),
        "norm2_gain": jnp.clip(1.0 + 0.1 * jax.random.normal(arg_keys[12], (D,), jnp.float32), 0.5, 1.5).astype(jnp.bfloat16),
        "norm2_shift": noise(arg_keys[13], (D,), 0.2, 1.1953125, ((0, 8),)),
        "bias_table": noise(arg_keys[14], (RPB_ROWS, HEADS), 0.5, 3.0, ((1, 8),)),
        "rel_index": draw_rel_index(jax.random.fold_in(arg_keys[17], 71), 0),
        "cotangent": noise(arg_keys[16], (CLIPS, FRAMES, HEIGHT, WIDTH, D), 1.0, 6.0, ((0, 4), (1, 4), (2, 2))),
    }


@jax.custom_vjp
def low(v):
    return lax.optimization_barrier(v.astype(jnp.bfloat16)).astype(jnp.float32)

@jax.custom_vjp
def low_back(v):
    return v

def low_keep(v):
    return (low(v), None)

def low_pass(kept, grad):
    return (grad,)

def back_keep(v):
    return (v, None)

def back_low(kept, grad):
    return (low(grad),)
low.defvjp(low_keep, low_pass)
low_back.defvjp(back_keep, back_low)
precise = lax.Precision.HIGHEST

def layer_norm(values, norm_gain, norm_shift):
    centre = values - lax.optimization_barrier(jnp.mean(values, axis=-1, keepdims=True))
    inv_std = lax.rsqrt(lax.optimization_barrier(jnp.mean(centre * centre, axis=-1, keepdims=True)) + 1e-05)
    return centre * inv_std * norm_gain + norm_shift

def rolled_regions():
    frame_pos = jnp.arange(FRAMES)
    row_pos = jnp.arange(HEIGHT)
    column_pos = jnp.arange(WIDTH)
    frame_reg = (frame_pos >= FRAMES - WIN_T).astype(jnp.int32) + (frame_pos >= FRAMES - SHIFT_T).astype(jnp.int32)
    row_reg = (row_pos >= HEIGHT - WIN_H).astype(jnp.int32) + (row_pos >= HEIGHT - SHIFT_H).astype(jnp.int32)
    column_reg = (column_pos >= WIDTH - WIN_W).astype(jnp.int32) + (column_pos >= WIDTH - SHIFT_W).astype(jnp.int32)
    return frame_reg[:, None, None] * 9 + row_reg[None, :, None] * 3 + column_reg[None, None, :]

def to_windows(positions):
    trailing_shape = positions.shape[3:]
    blocks = positions.reshape((FRAMES // WIN_T, WIN_T, HEIGHT // WIN_H, WIN_H, WIDTH // WIN_W, WIN_W) + trailing_shape)
    axes_order = (0, 2, 4, 1, 3, 5) + tuple(range(6, 6 + len(trailing_shape)))
    return blocks.transpose(axes_order).reshape((-1, WIN) + trailing_shape)

def from_windows(windows):
    blocks = windows.reshape(FRAMES // WIN_T, HEIGHT // WIN_H, WIDTH // WIN_W, WIN_T, WIN_H, WIN_W, windows.shape[-1])
    return blocks.transpose(0, 3, 1, 4, 2, 5, 6).reshape(FRAMES, HEIGHT, WIDTH, windows.shape[-1])

def clip_forward(clip_values, params, rel_index):
    qkv_w, query_b, value_b, proj_w, proj_b, fc1_w, fc1_b, fc2_w, fc2_b, gain_one, shift_one, gain_two, shift_two, table = params
    token_rows = clip_values.reshape(-1, D)
    entry_rows = low(layer_norm(token_rows, gain_one, shift_one))
    projected = jnp.dot(entry_rows, qkv_w, precision=precise)
    queries = low(low_back(projected[:, :D] + query_b))
    keys_rows = low(low_back(projected[:, D:2 * D]))
    values_rows = low(low_back(projected[:, 2 * D:] + value_b))

    def windowed(values):
        rolled = jnp.roll(values.reshape(FRAMES, HEIGHT, WIDTH, D), (-SHIFT_T, -SHIFT_H, -SHIFT_W), axis=(0, 1, 2))
        return to_windows(rolled)
    region_win = to_windows(rolled_regions()[..., None])[..., 0]
    position_bias = table[rel_index].transpose(2, 0, 1)

    def one_window(inputs):
        query_win, key_win, value_win, region = inputs
        query_head = query_win.reshape(WIN, HEADS, HEAD_DIM)
        key_head = key_win.reshape(WIN, HEADS, HEAD_DIM)
        value_head = value_win.reshape(WIN, HEADS, HEAD_DIM)
        logits = low_back(jnp.einsum('qhd,khd->hqk', query_head, key_head, precision=precise))
        masked = jnp.where(region[:, None] != region[None, :], -100.0, 0.0)
        logits = logits * HEAD_DIM ** (-0.5) + position_bias + masked
        weights = low(jax.nn.softmax(logits, axis=-1))
        mixture = jnp.einsum('hqk,khd->qhd', weights, value_head, precision=precise).reshape(WIN, D)
        return low(low_back(mixture))
    attended = lax.map(jax.checkpoint(one_window), (windowed(queries), windowed(keys_rows), windowed(values_rows), region_win))
    back_rows = jnp.roll(from_windows(attended), (SHIFT_T, SHIFT_H, SHIFT_W), axis=(0, 1, 2)).reshape(-1, D)
    attention = low_back(jnp.dot(back_rows, proj_w, precision=precise)) + proj_b
    middle = token_rows + attention
    second = low(layer_norm(middle, gain_two, shift_two))
    hidden = low_back(jnp.dot(second, fc1_w, precision=precise)) + fc1_b
    activation = low(jax.nn.gelu(hidden, approximate=False))
    branch = low_back(jnp.dot(activation, fc2_w, precision=precise)) + fc2_b
    return (middle + branch).reshape(FRAMES, HEIGHT, WIDTH, D)

def reference(tokens, qkv_weight, query_bias, value_bias, proj_weight, proj_bias, fc1_weight, fc1_bias, fc2_weight, fc2_bias, norm1_gain, norm1_shift, norm2_gain, norm2_shift, bias_table, rel_index, cotangent):
    params = jax.tree.map(lambda member: member.astype(jnp.float32), (qkv_weight, query_bias, value_bias, proj_weight, proj_bias, fc1_weight, fc1_bias, fc2_weight, fc2_bias, norm1_gain, norm1_shift, norm2_gain, norm2_shift, bias_table))
    initial = jax.tree.map(jnp.zeros_like, params)

    def per_clip(running, inputs):
        clip_values, grad_out = inputs
        outputs, pullback = jax.vjp(lambda values, weights: clip_forward(values, weights, rel_index), clip_values, params)
        grad_in, grad_params = pullback(grad_out)
        return (jax.tree.map(jnp.add, running, grad_params), (outputs.astype(jnp.bfloat16), grad_in))
    totals, stacked = lax.scan(per_clip, initial, (tokens.astype(jnp.float32), cotangent.astype(jnp.float32)))
    return (stacked[0], stacked[1], totals[0], totals[1], totals[2], totals[3], totals[4], totals[5], totals[6], totals[7], totals[8], totals[9], totals[10], totals[11], totals[12], totals[13])
```

```python
import jax
import jax.numpy as jnp
import numpy as np
from jax import lax
from jax.experimental import pallas as pl
from jax.experimental.pallas import tpu as pltpu
from jax.sharding import PartitionSpec as P

D = 512
HEADS = 16
FF = 2048
WIN_T = 8
WIN_H = 7
WIN_W = 7
HEAD_DIM = 32
SHIFT_T = 4
SHIFT_H = 3
SHIFT_W = 3
WIDTH = 14
WIN = 392
RPB_ROWS = 2535

ROWS = 400
LANES = 128
GROUP = LANES // HEAD_DIM
CELLS = WIN_H * WIN_W
CELL_ROWS = 56
CELL_LANES = 64
DIFF_T = 2 * WIN_T - 1
DIFF_HW = (2 * WIN_H - 1) * (2 * WIN_W - 1)
SPAN = WIN_T * CELL_LANES
WIDE = 2 * SPAN
LOG2E = 1.4426950408889634
SCALE = HEAD_DIM**-0.5

f32 = jnp.float32
bf16 = jnp.bfloat16
NN = (((1,), (0,)), ((), ()))
NT = (((1,), (1,)), ((), ()))
TN = (((0,), (0,)), ((), ()))


def mm(left, right, dims):
    return lax.dot_general(left, right, dims, preferred_element_type=f32)


def flipped(value, axis, bit):
    devices = lax.axis_size(axis)
    return lax.ppermute(value, axis, [(i, i ^ bit) for i in range(devices)])


def bits_of(axis):
    count = lax.axis_size(axis)
    assert count & (count - 1) == 0
    return [1 << n for n in range(count.bit_length() - 1)]


def both_orders(mine, theirs, axis, bit):
    high = (lax.axis_index(axis) & bit) != 0
    return jnp.stack([jnp.where(high, theirs, mine), jnp.where(high, mine, theirs)])


def doubled(value, steps):
    for axis, bit in steps:
        value = both_orders(value, flipped(value, axis, bit), axis, bit)
    return value


def tile_steps():
    ta_bits = bits_of("ta")
    return [("ta", b) for b in ta_bits[1:]] + [("ha", b) for b in bits_of("ha")] + [("ta", b) for b in ta_bits[:1]]


def ordered(value, steps, axes):
    got = list(reversed(steps))
    want = [(axis, b) for axis in axes for b in reversed(bits_of(axis))]
    lead = len(got)
    order = [got.index(w) for w in want]
    value = value.transpose(order + list(range(lead, value.ndim)))
    sizes = [lax.axis_size(axis) for axis in axes]
    return value.reshape(sizes + list(value.shape[lead:]))


def summed_share(value, low):
    ta_bits = bits_of("ta")
    ha_bits = bits_of("ha")
    names = [("ta", b) for b in reversed(ta_bits)] + [("ha", b) for b in reversed(ha_bits)]
    value = value.reshape((2,) * len(names) + value.shape[1:])
    for axis, bit in [("ta", b) for b in ta_bits[:1]] + [("ha", b) for b in ha_bits] + [("ta", b) for b in ta_bits[1:]]:
        at = names.index((axis, bit))
        high = jnp.where((lax.axis_index(axis) & bit) != 0, 1, 0)
        keep = lax.dynamic_index_in_dim(value, high, at, keepdims=False)
        send = lax.dynamic_index_in_dim(value, 1 - high, at, keepdims=False)
        if low:
            send = send.astype(bf16)
        value = keep + flipped(send, axis, bit).astype(f32)
        names.pop(at)
    return value


def summed_col(value, low):
    for bit in bits_of("col"):
        if low:
            value = value.astype(bf16)
        value = value.astype(f32) + flipped(value, "col", bit).astype(f32)
    return value


def rank_shifted(value, ta_by, ha_by):
    n_ta, n_ha = lax.axis_size("ta"), lax.axis_size("ha")
    pairs = [
        (t * n_ha + h, ((t + ta_by) % n_ta) * n_ha + (h + ha_by) % n_ha) for t in range(n_ta) for h in range(n_ha)
    ]
    return lax.ppermute(value, ("ta", "ha"), pairs)


def moved(piece, ta_by, ha_by):
    shape = piece.shape
    return rank_shifted(piece.reshape(-1, D), ta_by, ha_by).reshape(shape)


def windows_in(tile):
    clips = tile.shape[0]
    t, h = SHIFT_T, SHIFT_H
    own = tile[:, t:, h:]
    down = moved(tile[:, t:, :h], 0, -1)
    ahead = moved(tile[:, :t, h:], -1, 0)
    corner = moved(tile[:, :t, :h], -1, -1)
    grid = jnp.concatenate(
        [jnp.concatenate([own, down], axis=2), jnp.concatenate([ahead, corner], axis=2)], axis=1
    )
    left = grid[:, :, :, SHIFT_W : SHIFT_W + WIN_W]
    right = jnp.concatenate([grid[:, :, :, SHIFT_W + WIN_W :], grid[:, :, :, :SHIFT_W]], axis=3)
    rows = jnp.stack([left, right], axis=1).reshape(2 * clips, WIN, D)
    return jnp.pad(rows, ((0, 0), (0, ROWS - WIN), (0, 0)))


def windows_out(rows, clips):
    t, h = SHIFT_T, SHIFT_H
    grid = rows[:, :WIN].reshape(clips, 2, WIN_T, WIN_H, WIN_W, D)
    left, right = grid[:, 0], grid[:, 1]
    cut = WIN_W - SHIFT_W
    grid = jnp.concatenate([right[:, :, :, cut:], left, right[:, :, :, :cut]], axis=3)
    kind = rows.dtype
    down = moved(grid[:, :t, WIN_H - h :].astype(bf16), 0, 1).astype(kind)
    ahead = moved(grid[:, t:, : WIN_H - h].astype(bf16), 1, 0).astype(kind)
    corner = moved(grid[:, t:, WIN_H - h :].astype(bf16), 1, 1).astype(kind)
    own = grid[:, :t, : WIN_H - h]
    return jnp.concatenate(
        [jnp.concatenate([corner, ahead], axis=2), jnp.concatenate([down, own], axis=2)], axis=1
    )


def cell_one_hot():
    cell = np.arange(CELLS)
    r, c = cell // WIN_W, cell % WIN_W
    diff = (r[:, None] - r[None, :] + WIN_H - 1) * (2 * WIN_W - 1) + c[:, None] - c[None, :] + WIN_W - 1
    diff = np.pad(diff, ((0, 0), (0, CELL_LANES - CELLS)), constant_values=-1).reshape(-1)
    return jnp.asarray(diff, jnp.int32)[None, :] == lax.broadcasted_iota(jnp.int32, (DIFF_HW, diff.size), 0)


def packed_position(index):
    return index // CELLS, index % CELLS


def row_picker(rows_first):
    shape = (ROWS, WIN_T * CELL_ROWS) if rows_first else (WIN_T * CELL_ROWS, ROWS)
    i = lax.broadcasted_iota(jnp.int32, shape, 0 if rows_first else 1)
    p = lax.broadcasted_iota(jnp.int32, shape, 1 if rows_first else 0)
    frame, cell = packed_position(i)
    return jnp.where((p == frame * CELL_ROWS + cell) & (i < WIN), 1.0, 0.0).astype(bf16)


def lane_picker(padded_first):
    shape = (SPAN, ROWS) if padded_first else (ROWS, SPAN)
    j = lax.broadcasted_iota(jnp.int32, shape, 1 if padded_first else 0)
    p = lax.broadcasted_iota(jnp.int32, shape, 0 if padded_first else 1)
    frame, cell = packed_position(j)
    return jnp.where((p == frame * CELL_LANES + cell) & (j < WIN), 1.0, 0.0).astype(bf16)


def bias_kernel(cells_ref, rows_ref, lanes_ref, bias_ref):
    cells = cells_ref[0].astype(f32)
    frames = []
    for frame in range(WIN_T):
        start = (WIN_T - 1 - frame) * CELL_LANES
        frames.append(pltpu.roll(cells, (WIDE - start) % WIDE, 1)[:, :SPAN].astype(bf16))
    picked = jnp.zeros((ROWS, SPAN), f32)
    for frame in range(WIN_T):
        picked = picked + mm(rows_ref[frame], frames[frame], NN)
    bias_ref[0] = mm(picked.astype(bf16), lanes_ref[...], NN) * LOG2E


def expanded_bias(cells):
    rows = row_picker(True).reshape(ROWS, WIN_T, CELL_ROWS).transpose(1, 0, 2)
    return pl.pallas_call(
        bias_kernel,
        grid=(HEADS,),
        in_specs=[
            pl.BlockSpec((1, CELL_ROWS, WIDE), lambda h: (h, 0, 0)),
            pl.BlockSpec((WIN_T, ROWS, CELL_ROWS), lambda h: (0, 0, 0)),
            pl.BlockSpec((SPAN, ROWS), lambda h: (0, 0)),
        ],
        out_specs=pl.BlockSpec((1, ROWS, ROWS), lambda h: (h, 0, 0)),
        out_shape=jax.ShapeDtypeStruct((HEADS, ROWS, ROWS), f32),
        name="bias_expand",
    )(cells, rows, lane_picker(True))


def halves(value):
    high = value.astype(bf16)
    return high, (value - high.astype(f32)).astype(bf16)


def bias_grad_kernel(grad_ref, rows_ref, lanes_ref, cells_ref):
    total = jnp.zeros((CELL_ROWS, WIDE), f32)
    high, low = halves(grad_ref[0])
    spread = mm(high, lanes_ref[...], NN) + mm(low, lanes_ref[...], NN)
    high, low = halves(spread)
    for frame in range(WIN_T):
        picked = mm(rows_ref[frame], high, NN) + mm(rows_ref[frame], low, NN)
        picked = jnp.concatenate([picked, jnp.zeros((CELL_ROWS, SPAN), f32)], axis=1)
        total = total + pltpu.roll(picked, (WIN_T - 1 - frame) * CELL_LANES, 1)
    cells_ref[0] = total


def collected_bias_grad(grad):
    rows = row_picker(False).reshape(WIN_T, CELL_ROWS, ROWS)
    return pl.pallas_call(
        bias_grad_kernel,
        grid=(HEADS,),
        in_specs=[
            pl.BlockSpec((1, ROWS, ROWS), lambda h: (h, 0, 0)),
            pl.BlockSpec((WIN_T, CELL_ROWS, ROWS), lambda h: (0, 0, 0)),
            pl.BlockSpec((ROWS, SPAN), lambda h: (0, 0)),
        ],
        out_specs=pl.BlockSpec((1, CELL_ROWS, WIDE), lambda h: (h, 0, 0)),
        out_shape=jax.ShapeDtypeStruct((HEADS, CELL_ROWS, WIDE), f32),
        name="bias_collect",
    )(grad, rows, lane_picker(False))


def difference_rows(rel_index):
    dt = np.arange(DIFF_T)[::-1] - (WIN_T - 1)
    dr = np.arange(2 * WIN_H - 1) - (WIN_H - 1)
    dc = np.arange(2 * WIN_W - 1) - (WIN_W - 1)
    t, r, c = np.meshgrid(dt, dr, dc, indexing="ij")

    def place(sign):
        a, b, d = (np.maximum(sign * v, 0) for v in (t, r, c))
        return ((a * WIN_H + b) * WIN_W + d).reshape(-1)

    flat = place(1) * WIN + place(-1)
    return rel_index.reshape(-1)[jnp.asarray(flat, jnp.int32)]


def forward_kernel(q_ref, k_ref, v_ref, ask_ref, tell_ref, bias_ref, mix_ref, inv_ref, exp_ref):
    group = lax.broadcasted_iota(jnp.int32, (ROWS, LANES), 1) // HEAD_DIM
    q, k, v = q_ref[0], k_ref[0], v_ref[0]
    ask, tell = ask_ref[0], tell_ref[0]
    zero = jnp.zeros((ROWS, LANES), bf16)
    one = jnp.ones((ROWS, LANES), bf16)
    for h in range(GROUP):
        own = group == h
        spare = group == (h + 1) % GROUP
        q_h = jnp.where(own, q, jnp.where(spare, ask, zero))
        k_h = jnp.where(own, k, jnp.where(spare, tell, zero))
        v_h = jnp.where(own, v, one)
        scores = mm(q_h, k_h, NT) + bias_ref[h]
        exponent = jnp.exp2(scores - jnp.max(scores, axis=1, keepdims=True)).astype(bf16)
        exp_ref[0, h] = exponent
        mixed = mm(exponent, v_h, NN)
        inverse = 1.0 / pltpu.roll(mixed, HEAD_DIM, 1)
        mixture = (mixed * inverse).astype(bf16)
        if h == 0:
            mix_ref[0] = mixture
            inv_ref[0] = inverse
        else:
            mix_ref[0] = jnp.where(own, mixture, mix_ref[0])
            inv_ref[0] = jnp.where(own, inverse, inv_ref[0])


def head_block(offset):
    return pl.BlockSpec((1, ROWS, LANES), lambda g, w: (w, 0, g + offset))


def attention_forward(qkv, ask, tell, bias):
    wins = qkv.shape[0]
    per_group = D // LANES
    pair = pl.BlockSpec((1, ROWS, LANES), lambda g, w: (w, 0, 0))
    return pl.pallas_call(
        forward_kernel,
        grid=(per_group, wins),
        in_specs=[
            head_block(0),
            head_block(per_group),
            head_block(2 * per_group),
            pair,
            pair,
            pl.BlockSpec((GROUP, ROWS, ROWS), lambda g, w: (g, 0, 0)),
        ],
        out_specs=[
            head_block(0),
            head_block(0),
            pl.BlockSpec((1, GROUP, ROWS, ROWS), lambda g, w: (w, g, 0, 0)),
        ],
        out_shape=[
            jax.ShapeDtypeStruct((wins, ROWS, D), bf16),
            jax.ShapeDtypeStruct((wins, ROWS, D), f32),
            jax.ShapeDtypeStruct((wins, HEADS, ROWS, ROWS), bf16),
        ],
        name="attention_forward",
    )(qkv, qkv, qkv, ask, tell, bias)


def backward_kernel(
    q_ref, k_ref, v_ref, mix_ref, inv_ref, exp_ref, grad_ref, dq_ref, dk_ref, dv_ref, bias_ref
):
    win = pl.program_id(1)
    lane = lax.broadcasted_iota(jnp.int32, (ROWS, LANES), 1)
    group, within = lane // HEAD_DIM, lane % HEAD_DIM
    q, k, v = q_ref[0], k_ref[0], v_ref[0]
    inverse = inv_ref[0]
    grad = grad_ref[0].astype(f32)
    side_a = lax.broadcasted_iota(jnp.int32, (LANES, LANES), 0) // HEAD_DIM
    side_b = lax.broadcasted_iota(jnp.int32, (LANES, LANES), 1) // HEAD_DIM
    same = jnp.where(side_a == side_b, 1.0, 0.0).astype(bf16)
    high, low = halves(grad * mix_ref[0].astype(f32))
    drop = pltpu.roll((mm(high, same, NN) + mm(low, same, NN)) * inverse, HEAD_DIM, 1)
    high, low = halves(-drop)
    zero = jnp.zeros((ROWS, LANES), bf16)
    ask = jnp.where(within == 0, high, jnp.where(within == 1, low, zero))
    tell = jnp.where(within < 2, jnp.ones((ROWS, LANES), bf16), zero)
    scaled = (grad * inverse).astype(bf16)
    for h in range(GROUP):
        own = group == h
        spare = group == (h + 1) % GROUP
        grad_h = jnp.where(own, scaled, jnp.where(spare, ask, zero))
        v_h = jnp.where(own, v, jnp.where(spare, tell, zero))
        exponent = exp_ref[0, h]
        grad_scores = exponent.astype(f32) * mm(grad_h, v_h, NT)

        @pl.when(win == 0)
        def _():
            bias_ref[h] = grad_scores

        @pl.when(win != 0)
        def _():
            bias_ref[h] += grad_scores

        low_scores = grad_scores.astype(bf16)
        dq = (mm(low_scores, k, NN) * SCALE).astype(bf16)
        dk = (mm(low_scores, q, TN) * (1.0 / LOG2E)).astype(bf16)
        dv = mm(exponent, scaled, TN).astype(bf16)
        if h == 0:
            dq_ref[0], dk_ref[0], dv_ref[0] = dq, dk, dv
        else:
            dq_ref[0] = jnp.where(own, dq, dq_ref[0])
            dk_ref[0] = jnp.where(own, dk, dk_ref[0])
            dv_ref[0] = jnp.where(own, dv, dv_ref[0])


def attention_backward(qkv, mixture, inverse, exponent, grad):
    wins = qkv.shape[0]
    per_group = D // LANES
    return pl.pallas_call(
        backward_kernel,
        grid=(per_group, wins),
        in_specs=[
            head_block(0),
            head_block(per_group),
            head_block(2 * per_group),
            head_block(0),
            head_block(0),
            pl.BlockSpec((1, GROUP, ROWS, ROWS), lambda g, w: (w, g, 0, 0)),
            head_block(0),
        ],
        out_specs=[head_block(0)] * 3 + [pl.BlockSpec((GROUP, ROWS, ROWS), lambda g, w: (g, 0, 0))],
        out_shape=[jax.ShapeDtypeStruct((wins, ROWS, D), bf16)] * 3
        + [jax.ShapeDtypeStruct((HEADS, ROWS, ROWS), f32)],
        name="attention_backward",
    )(qkv, qkv, qkv, mixture, inverse, exponent, grad)


def mask_pairs(clips):
    index = np.arange(ROWS)
    frame, cell = packed_position(index)
    late_t = jnp.asarray((frame >= WIN_T - SHIFT_T).astype(np.int32))
    late_r = jnp.asarray((cell // WIN_W >= WIN_H - SHIFT_H).astype(np.int32))
    late_c = jnp.asarray((cell % WIN_W >= WIN_W - SHIFT_W).astype(np.int32))
    last_t = (lax.axis_index("ta") == lax.axis_size("ta") - 1).astype(jnp.int32)
    last_r = (lax.axis_index("ha") == lax.axis_size("ha") - 1).astype(jnp.int32)
    base = late_t * last_t * 4 + late_r * last_r * 2
    region = jnp.stack([base, base + late_c])[:, :, None]
    lane = lax.broadcasted_iota(jnp.int32, (2, ROWS, LANES), 2) % HEAD_DIM
    real = lax.broadcasted_iota(jnp.int32, (2, ROWS, LANES), 1) < WIN
    full = np.float32(-100.0 * LOG2E)
    high = np.float32(full.astype(jnp.bfloat16))
    rest = np.float32(np.float64(-100.0 * LOG2E) - np.float64(high))
    ask = jnp.where(lane < 16, (lane % 8 == region).astype(f32), (lane == 16).astype(f32))
    apart = (lane % 8 != region) & real
    tell = jnp.where(
        lane < 8,
        jnp.where(apart, high, 0.0),
        jnp.where(lane < 16, jnp.where(apart, rest, 0.0), jnp.where((lane == 16) & ~real, -1e30, 0.0)),
    )
    return jnp.tile(ask.astype(bf16), (clips, 1, 1)), jnp.tile(tell.astype(bf16), (clips, 1, 1))


def norm_rows(values, norm_gain, norm_shift):
    centre = values - jnp.mean(values, axis=-1, keepdims=True)
    inv_std = lax.rsqrt(jnp.mean(centre * centre, axis=-1, keepdims=True) + 1e-05)
    normed = centre * inv_std
    return (normed, inv_std, normed * norm_gain + norm_shift)


def norm_back(grad_out, normed, inv_std, norm_gain):
    scaled = grad_out * norm_gain
    return inv_std * (
        scaled
        - jnp.mean(scaled, axis=-1, keepdims=True)
        - normed * jnp.mean(scaled * normed, axis=-1, keepdims=True)
    )


def gelu_slope(values):
    normal_cdf = 0.5 * (1.0 + lax.erf(values * 0.7071067811865476))
    return normal_cdf + values * jnp.exp(-0.5 * values * values) * 0.3989422804014327


def per_device(
    tokens,
    qkv_weight,
    query_bias,
    value_bias,
    proj_weight,
    proj_bias,
    fc1_weight,
    fc1_bias,
    fc2_weight,
    fc2_bias,
    norm1_gain,
    norm1_shift,
    norm2_gain,
    norm2_shift,
    bias_table,
    rel_index,
    cotangent,
):
    clips = tokens.shape[0]
    n_col = lax.axis_size("col")
    tiles = lax.axis_size("ta") * lax.axis_size("ha")
    steps = tile_steps()

    vectors = [
        query_bias,
        value_bias,
        proj_bias,
        fc1_bias,
        fc2_bias,
        norm1_gain,
        norm1_shift,
        norm2_gain,
        norm2_shift,
    ]
    heads_here = bias_table.shape[1]
    sizes = [v.shape[0] for v in vectors] + [RPB_ROWS * heads_here]
    small = jnp.concatenate(vectors + [bias_table.T.reshape(-1)])
    small_len = -(-small.shape[0] // LANES) * LANES
    small = jnp.pad(small, (0, small_len - small.shape[0])).reshape(-1, LANES)
    small_full = ordered(doubled(small, steps), steps, ("ta", "ha")).reshape(tiles, -1).astype(f32)
    cuts = np.cumsum([0] + sizes)
    parts = [small_full[:, a:b] for a, b in zip(cuts[:-1], cuts[1:])]
    (
        bias_query,
        bias_value,
        bias_proj,
        bias_fc1,
        bias_fc2,
        gain_one,
        shift_one,
        gain_two,
        shift_two,
    ) = [p.reshape(-1) for p in parts[:-1]]
    table = parts[-1].reshape(HEADS, RPB_ROWS)

    col_steps = [("col", b) for b in bits_of("col")]
    qkv_steps = col_steps + steps
    qkv_full = ordered(doubled(qkv_weight, qkv_steps), qkv_steps, ("col", "ta", "ha"))
    qkv_full = qkv_full.transpose(0, 3, 1, 2, 4).reshape(D, 3 * D)

    x_rows = windows_in(tokens).reshape(-1, D).astype(f32)
    wins = 2 * clips

    later = jnp.concatenate(
        [proj_weight.reshape(-1, LANES), fc1_weight.reshape(-1, LANES), fc2_weight.reshape(-1, LANES)]
    )
    later = lax.all_gather(later, ("col", "ta", "ha"), axis=0).reshape(n_col, tiles, -1, LANES)
    cuts = np.cumsum([0, proj_weight.size // LANES, fc1_weight.size // LANES, fc2_weight.size // LANES])

    def whole(at, shape):
        piece = later[:, :, cuts[at] : cuts[at + 1]].reshape((n_col, tiles) + shape)
        return piece.transpose(0, 2, 1, 3).reshape(n_col * shape[0], tiles * shape[1])

    proj_full = whole(0, proj_weight.shape)
    fc1_full = whole(1, fc1_weight.shape)
    fc2_full = whole(2, fc2_weight.shape)

    grad_out = windows_in(cotangent).reshape(-1, D)

    table_rows = difference_rows(rel_index)
    by_difference = jnp.take(table, table_rows, axis=1).astype(bf16).reshape(HEADS * DIFF_T, DIFF_HW)
    one_hot = cell_one_hot().astype(bf16)
    cells = mm(by_difference, one_hot, NN).astype(bf16)
    cells = cells.reshape(HEADS, DIFF_T, CELLS, CELL_LANES).transpose(0, 2, 1, 3)
    cells = jnp.pad(cells, ((0, 0), (0, CELL_ROWS - CELLS), (0, 1), (0, 0))).reshape(HEADS, CELL_ROWS, WIDE)
    position_bias = expanded_bias(cells)
    ask, tell = mask_pairs(clips)

    normed_one, inv_one, pre_one = norm_rows(x_rows, gain_one, shift_one)
    entry_rows = pre_one.astype(bf16)
    projected = jnp.dot(entry_rows, qkv_full, preferred_element_type=f32)
    offsets = jnp.concatenate([bias_query, jnp.zeros((D,), f32), bias_value])
    scales = jnp.concatenate([jnp.full((D,), SCALE * LOG2E, f32), jnp.ones((2 * D,), f32)])
    qkv = ((projected + offsets) * scales).astype(bf16).reshape(wins, ROWS, 3 * D)
    mixture, inverse, exponent = attention_forward(qkv, ask, tell, position_bias)
    mixture_rows = mixture.reshape(-1, D)
    middle = x_rows + (jnp.dot(mixture_rows, proj_full, preferred_element_type=f32) + bias_proj)
    normed_two, inv_two, pre_two = norm_rows(middle, gain_two, shift_two)
    second = pre_two.astype(bf16)
    hidden = jnp.dot(second, fc1_full, preferred_element_type=f32) + bias_fc1
    activation = jax.nn.gelu(hidden, approximate=False).astype(bf16)
    result = middle + (jnp.dot(activation, fc2_full, preferred_element_type=f32) + bias_fc2)
    block_out = windows_out(result.astype(bf16).reshape(wins, ROWS, D), clips)

    grad_fc2_bias = jnp.sum(grad_out.astype(f32), axis=0)
    grad_fc2_t = mm(grad_out, activation, TN)
    grad_act = mm(grad_out, fc2_full, NT)
    grad_hidden = grad_act * gelu_slope(hidden)
    grad_fc1_bias = jnp.sum(grad_hidden, axis=0)
    hidden_low = grad_hidden.astype(bf16)
    grad_fc1_t = mm(hidden_low, second, TN)
    grad_second = mm(hidden_low, fc1_full, NT)
    grad_gain_two = jnp.sum(grad_second * normed_two, axis=0)
    grad_shift_two = jnp.sum(grad_second, axis=0)
    grad_middle = grad_out.astype(f32) + norm_back(grad_second, normed_two, inv_two, gain_two)
    grad_proj_bias = jnp.sum(grad_middle, axis=0)
    middle_low = grad_middle.astype(bf16)
    grad_proj_t = mm(middle_low, mixture_rows, TN)
    grad_mixture = mm(middle_low, proj_full, NT).astype(bf16)

    early = jnp.concatenate(
        [
            grad_proj_t.astype(bf16).reshape(tiles, -1, D),
            grad_fc1_t.astype(bf16).reshape(tiles, -1, D),
            grad_fc2_t.astype(bf16).reshape(tiles, -1, D),
        ],
        axis=1,
    )
    early = lax.psum(lax.psum_scatter(early, ("ta", "ha"), scatter_dimension=0), "col").astype(f32)
    cuts = np.cumsum([0, D // tiles, FF // tiles, FF // tiles])
    share_proj = early[cuts[0] : cuts[1]].T
    share_fc1 = early[cuts[1] : cuts[2]].T
    share_fc2 = early[cuts[2] : cuts[3]].reshape(D // tiles, FF).T

    grad_q, grad_k, grad_v, bias_pairs = attention_backward(
        qkv, mixture, inverse, exponent, grad_mixture.reshape(wins, ROWS, D)
    )
    grad_queries, grad_keys, grad_values = [g.reshape(-1, D) for g in (grad_q, grad_k, grad_v)]
    grad_query_bias = jnp.sum(grad_queries.astype(f32), axis=0)
    grad_value_bias = jnp.sum(grad_values.astype(f32), axis=0)
    grad_qkv_t = jnp.concatenate([mm(g, entry_rows, TN) for g in (grad_queries, grad_keys, grad_values)])
    share_qkv = summed_col(summed_share(grad_qkv_t.reshape(tiles, -1, D), True), True).T

    cell_grads = collected_bias_grad(bias_pairs)[:, :CELLS, : DIFF_T * CELL_LANES]
    cell_grads = cell_grads.reshape(HEADS, CELLS, DIFF_T, CELL_LANES).transpose(0, 2, 1, 3)
    by_difference = lax.dot_general(
        cell_grads.reshape(HEADS * DIFF_T, CELLS * CELL_LANES),
        cell_one_hot().astype(f32),
        NT,
        precision=lax.Precision.HIGHEST,
        preferred_element_type=f32,
    ).reshape(HEADS, RPB_ROWS)

    grad_entry = (
        mm(grad_queries, qkv_full[:, :D], NT)
        + mm(grad_keys, qkv_full[:, D : 2 * D], NT)
        + mm(grad_values, qkv_full[:, 2 * D :], NT)
    )
    grad_gain_one = jnp.sum(grad_entry * normed_one, axis=0)
    grad_shift_one = jnp.sum(grad_entry, axis=0)
    grad_tokens = grad_middle + norm_back(grad_entry, normed_one, inv_one, gain_one)
    tokens_grad = windows_out(grad_tokens.reshape(wins, ROWS, D), clips)

    pieces = [
        grad_query_bias,
        grad_value_bias,
        grad_proj_bias,
        grad_fc1_bias,
        grad_fc2_bias,
        grad_gain_one,
        grad_shift_one,
        grad_gain_two,
        grad_shift_two,
        by_difference,
    ]
    flat = jnp.concatenate([p.reshape(tiles, -1) for p in pieces], axis=1)
    flat = jnp.pad(flat, ((0, 0), (0, small_len - flat.shape[1]))).reshape(tiles, -1, LANES)
    shares = summed_col(summed_share(flat, False), False).reshape(-1)
    cuts = np.cumsum([0] + sizes)
    outs = [shares[a:b] for a, b in zip(cuts[:-1], cuts[1:])]
    places = jnp.zeros((RPB_ROWS,), jnp.int32).at[table_rows].set(jnp.arange(RPB_ROWS, dtype=jnp.int32))
    share_table = jnp.take(outs[-1].reshape(heads_here, RPB_ROWS), places, axis=1).T

    return (
        block_out,
        tokens_grad,
        share_qkv,
        outs[0],
        outs[1],
        share_proj,
        outs[2],
        share_fc1,
        outs[3],
        share_fc2,
        outs[4],
        outs[5],
        outs[6],
        outs[7],
        outs[8],
        share_table,
    )


def solution(mesh):
    tile = P("col", "ta", "ha", None, None)
    weight = P("col", ("ta", "ha"))
    vector = P(("ta", "ha"))
    share = P(None, ("ta", "ha"))
    return jax.shard_map(
        per_device,
        mesh=mesh,
        in_specs=(
            tile,
            weight,
            vector,
            vector,
            weight,
            vector,
            weight,
            vector,
            weight,
            vector,
            vector,
            vector,
            vector,
            vector,
            share,
            P(),
            tile,
        ),
        out_specs=(
            tile,
            tile,
            share,
            vector,
            vector,
            share,
            vector,
            share,
            vector,
            share,
            vector,
            vector,
            vector,
            vector,
            vector,
            share,
        ),
        check_vma=False,
    )
```
